128 devices in a mesh: expert: 8 (over x, core), cuts: 16 (over y, z).
Axes of the slice: x: 4, y: 4, z: 4, core: 2. Of those that a mesh axis runs over, the one named last changes fastest.
Arguments:
- tokens: bfloat16 [1024, 4096], P('expert', 'cuts'), may hold values from -6 to 6
- routing: int32 [1024, 2], P('expert'), may hold values from 0 to 7, all different within a row; in each aligned block of 128 rows (0 to 127, 128 to 255, ...) at most 64 rows name the same one
- gates: float32 [1024, 2], P('expert'), may hold values from 0.2 to 1
- cotangent: bfloat16 [1024, 4096], P('expert', 'cuts'), may hold values from -6 to 6
- w_gate: bfloat16 [8, 4096, 8192], P('expert', None, 'cuts'), may hold values from -0.09375 to 0.09375
- w_up: bfloat16 [8, 4096, 8192], P('expert', None, 'cuts'), may hold values from -0.09375 to 0.09375
- w_down: bfloat16 [8, 8192, 4096], P('expert', 'cuts'), may hold values from -0.0625 to 0.0625
Outputs:
- mixed: bfloat16 [1024, 4096], P('expert', 'cuts')
- grad_tokens: bfloat16 [1024, 4096], P('expert', 'cuts')
- grad_gates: float32 [1024, 2], P('expert')
- grad_w_gate: bfloat16 [8, 4096, 8192], P('expert', None, 'cuts')
- grad_w_up: bfloat16 [8, 4096, 8192], P('expert', None, 'cuts')
- grad_w_down: bfloat16 [8, 8192, 4096], P('expert', 'cuts')
The draws below stay inside these ranges and needn't reach their ends.
Inputs may be any that keep to these rules, and one draw needn't show every extreme that they name: `routing`: in each aligned block of 128 rows (the tokens owned by one position along `expert`) no expert is named by more than 64 rows, a bound that some block reaches.
All inputs are finite; a program needn't handle non-finite values.
Results may differ from the reference program's by a relative error of at most 0.015.
Values may be sent and summed in bfloat16 or wider, within the bound.
A program may use at most 128 MiB of HBM per device.

```python
import math
import jax
import jax.numpy as jnp
import numpy as np
from jax import lax

D = 4096
FF = 8192
TOK_DEV = 128
EXPERTS = 8
CAP = 64
TOKENS = 1024
N_EXPERT = 8
N_CUTS = 16


def block_scale(own_key, shape, shards, low, high):
    level, own = 1.0, jax.random.fold_in(own_key, 6)
    for dim, blocks in shards:
        steps = jnp.exp(jax.random.uniform(jax.random.fold_in(own, dim), (blocks,), jnp.float32, low / len(shards), high / len(shards)))
        level = level * jnp.repeat(steps, shape[dim] // blocks).reshape([-1 if axis == dim else 1 for axis in range(len(shape))])
    return level


def routed_block(stream_key, own, number, rows, amount, top, bound, lean):
    order = jax.random.permutation(stream_key, amount)
    packed, common = load_shares(amount, rows * top, bound, lean, True), load_shares(amount, rows * top, bound, lean, False)
    places = jnp.arange(amount)

    def named(lengths, offset_by):
        used = int((lengths > 0).sum())
        fixed = max(1, used // 4)
        passed = fixed + (places - fixed + offset_by * (used - fixed)) % max(1, amount - fixed)
        return jnp.zeros((amount,), jnp.int32).at[order[jnp.where(places < fixed, places, passed)]].set(jnp.asarray(lengths, jnp.int32))

    lengths = jnp.where(number % 4 == 0, named(packed, number // 4), named(common, number - number // 4 - 1))
    mixed = jax.random.permutation(jax.random.fold_in(own, 3), amount)
    donor, receiver = mixed[0:amount // 2 * 2:2], mixed[1:amount // 2 * 2:2]
    margin = jnp.minimum(lengths[donor] - 1, bound - lengths[receiver]) // 2
    margin = jnp.where((donor == order[0]) | (receiver == order[0]) | (lengths[receiver] == 0), 0, jnp.maximum(margin, 0))
    passed = jax.random.randint(jax.random.fold_in(own, 4), (amount // 2,), 0, 1 << 20) % (margin + 1)
    lengths = lengths.at[donor].add(-passed).at[receiver].add(passed)
    members = jnp.searchsorted(jnp.cumsum(lengths), jnp.arange(rows * top), side="right").astype(jnp.int32)
    table = members.reshape(top, rows).T
    table = table[jax.random.permutation(jax.random.fold_in(own, 1), rows)]
    offset_by = jax.random.randint(jax.random.fold_in(own, 2), (rows, 1), 0, top)
    return jnp.take_along_axis(table, (jnp.arange(top)[None, :] + offset_by) % top, axis=1)


def load_shares(number_of, total, most, skew, full):
    loads = [(1 << 20) // math.isqrt(grade ** skew) + 1 for grade in range(1, number_of + 1)]
    largest = most if full else min(most, max(-(-total // number_of), total * loads[0] // sum(loads)))
    least = 1 if total - largest >= number_of - 1 else 0
    given, surplus = [largest] + [least] * (number_of - 1), total - largest - least * (number_of - 1)
    while surplus > 0:
        movable = [i for i in range(1, number_of) if given[i] < largest] or [i for i in range(1, number_of) if given[i] < most]
        mass, remaining = sum([loads[i] for i in movable]), surplus
        for i in movable:
            extra = min(most - given[i], max(1, remaining * loads[i] // mass), surplus)
            given[i] = given[i] + extra
            surplus = surplus - extra
    return np.array(given)


def bell_draw(stream_key, extent, deviation, most, pieces=(), kind=jnp.bfloat16):
    gain = block_scale(stream_key, extent, pieces, -0.22, 0.18) if pieces else 1.0
    values = jax.random.normal(stream_key, extent, jnp.float32) * deviation * gain
    return jnp.minimum(jnp.maximum(values, -most), most).astype(kind)


def setup_inputs(seed: int = 0) -> dict:
    key_of = jax.random.split(jax.random.key(seed), 8)
    tokens = bell_draw(key_of[0], (TOKENS, D), 1.0, 6.0, ((0, 8), (1, 16)))
    routing_keys = jax.random.split(jax.random.fold_in(key_of[1], 1), TOKENS // TOK_DEV)
    routing_turns = jax.random.permutation(jax.random.fold_in(key_of[1], 3), TOKENS // TOK_DEV)
    routing = jax.vmap(lambda own, number: routed_block(jax.random.fold_in(key_of[1], 2), own, number, TOK_DEV, EXPERTS, 2, CAP, 2))(routing_keys, routing_turns).reshape((TOKENS, 2))
    gates = jnp.clip(0.2 + 0.8 * jax.random.uniform(key_of[2], (TOKENS, 2), jnp.float32) ** block_scale(key_of[2], (TOKENS, 2), ((0, 8),), -0.2, 0.2), 0.2, 1.0)
    cotangent = bell_draw(key_of[3], (TOKENS, D), 1.0, 6.0, ((0, 8), (1, 16)))
    w_gate = bell_draw(key_of[4], (EXPERTS, D, FF), D ** -0.5, 0.09375, ((0, 8), (2, 16)))
    w_up = bell_draw(key_of[5], (EXPERTS, D, FF), D ** -0.5, 0.09375, ((0, 8), (2, 16)))
    w_down = bell_draw(key_of[6], (EXPERTS, FF, D), FF ** -0.5, 0.0625, ((0, 8), (1, 16)))
    return {"tokens": tokens, "routing": routing, "gates": gates, "cotangent": cotangent, "w_gate": w_gate, "w_up": w_up, "w_down": w_down}


def slot_destination(routing, experts, capacity):
    row_count = routing.shape[0]
    flat_route = routing.reshape(-1)
    onehot = (flat_route[:, None] == jnp.arange(experts, dtype=jnp.int32)[None, :]).astype(jnp.int32)
    before = jnp.cumsum(onehot, axis=0) - onehot
    position = jnp.sum(before * onehot, axis=1)
    return (flat_route * capacity + position).reshape(row_count, 2)


def cut_sum(lefts, rights, width):
    rows_here = lefts[0].shape[0]
    cols_here = rights[0].shape[1]

    def add_slice(index, summed):
        start = (index * width).astype(jnp.int32)
        term = jnp.zeros((rows_here, cols_here), jnp.float32)
        for left, right in zip(lefts, rights):
            term = term + jnp.dot(lax.dynamic_slice_in_dim(left, start, width, 1), lax.dynamic_slice_in_dim(right, start, width, 0), preferred_element_type=jnp.float32)
        rounded = lax.optimization_barrier(term.astype(jnp.bfloat16))
        return summed + rounded.astype(jnp.float32)

    initial = jnp.zeros((rows_here, cols_here), jnp.float32)
    return lax.fori_loop(0, N_CUTS, add_slice, initial).astype(jnp.bfloat16)


def one_expert(operands):
    x_rows, d_rows, gate_w, up_w, down_w = operands
    width = FF // N_CUTS
    gate_pre = jnp.dot(x_rows, gate_w, preferred_element_type=jnp.float32)
    up_pre = jnp.dot(x_rows, up_w, preferred_element_type=jnp.float32)
    sigmoid_gate = jax.nn.sigmoid(gate_pre)
    activated = gate_pre * sigmoid_gate
    hidden = (activated * up_pre).astype(jnp.bfloat16)
    expert_out = cut_sum((hidden,), (down_w,), width)
    grad_hidden = jnp.dot(d_rows, down_w.T, preferred_element_type=jnp.float32)
    grad_gate_pre = (grad_hidden * up_pre * sigmoid_gate * (1.0 + gate_pre * (1.0 - sigmoid_gate))).astype(jnp.bfloat16)
    grad_up_pre = (grad_hidden * activated).astype(jnp.bfloat16)
    grad_rows = cut_sum((grad_gate_pre, grad_up_pre), (gate_w.T, up_w.T), width)
    grad_down = jnp.dot(hidden.T, d_rows, preferred_element_type=jnp.float32).astype(jnp.bfloat16)
    grad_gate_w = jnp.dot(x_rows.T, grad_gate_pre, preferred_element_type=jnp.float32).astype(jnp.bfloat16)
    grad_up_w = jnp.dot(x_rows.T, grad_up_pre, preferred_element_type=jnp.float32).astype(jnp.bfloat16)
    return expert_out, grad_rows, grad_gate_w, grad_up_w, grad_down


def reference(tokens, routing, gates, cotangent, w_gate, w_up, w_down):
    groups = N_EXPERT
    blocks = routing.reshape(groups, TOK_DEV, 2)
    destination = jax.vmap(lambda block: slot_destination(block, EXPERTS, CAP))(blocks)
    expert_index = routing.reshape(-1).astype(jnp.int32)
    position = destination.reshape(-1).astype(jnp.int32) - expert_index * CAP
    owner_group = jnp.repeat(jnp.arange(groups, dtype=jnp.int32), TOK_DEV * 2)
    buffer_row = (owner_group * CAP + position).astype(jnp.int32)
    grad_out = cotangent.astype(jnp.float32)
    grad_pairs = (gates[:, :, None] * grad_out[:, None, :]).astype(jnp.bfloat16).reshape(-1, D)
    x_pairs = jnp.repeat(tokens, 2, axis=0)
    x_buffer = jnp.zeros((EXPERTS, groups * CAP, D), jnp.bfloat16).at[expert_index, buffer_row].set(x_pairs)
    d_buffer = jnp.zeros((EXPERTS, groups * CAP, D), jnp.bfloat16).at[expert_index, buffer_row].set(grad_pairs)
    expert_out, grad_rows, grad_gate_w, grad_up_w, grad_down = lax.map(one_expert, (x_buffer, d_buffer, w_gate, w_up, w_down))
    picked_out = expert_out[expert_index, buffer_row].reshape(TOKENS, 2, D).astype(jnp.float32)
    picked_grad = grad_rows[expert_index, buffer_row].reshape(TOKENS, 2, D).astype(jnp.float32)
    mixed = jnp.sum(gates[:, :, None] * picked_out, axis=1).astype(jnp.bfloat16)
    grad_tokens = jnp.sum(gates[:, :, None] * picked_grad, axis=1).astype(jnp.bfloat16)
    grad_gates = jnp.sum(grad_out[:, None, :] * picked_out, axis=2)
    return mixed, grad_tokens, grad_gates, grad_gate_w, grad_up_w, grad_down
```

```python
import functools

import jax
import jax.numpy as jnp
from jax import lax
from jax.experimental import pallas as pl
from jax.experimental.pallas import tpu as pltpu
from jax.sharding import PartitionSpec as P

MESH = pl.DeviceIdType.MESH
BF = jnp.bfloat16
F32 = jnp.float32
N = 4
SLOT = 64
TB = 128
FW = 256
HID = 512
ORDER = ((0, 1, 2), (1, 2, 0), (2, 0, 1))
ROWS_X = ((0, 48), (48, 48), (96, 32))
ROWS_C = ((0, 48), (48, 32), (80, 48))


def dot(a, b):
    return jnp.dot(a, b, preferred_element_type=F32)


def dot_nt(a, b):
    return lax.dot_general(a, b, (((1,), (1,)), ((), ())), preferred_element_type=F32)


def dot_tn(a, b):
    return lax.dot_general(a, b, (((0,), (0,)), ((), ())), preferred_element_type=F32)


def layer_kernel(
    x_in, c_in, route_in, gates_in, wg_in, wu_in, wd_in,
    mixed_out, gtok_out, ggate_out, xr_out, dr_out, hid_out, ggp_out, gup_out,
    gx, gc, xr, dr, sx, sc, wg, wu, wd, fa, fb, fh, fg, hid, ggp, gup,
    lm0, lm1, lm2, lg0, lg1, lg2, meta, mine, pick, back, gslot, qy, qz, qe,
    send_sem, recv_sem, local_sem,
):
    ei, ci = lax.axis_index("expert"), lax.axis_index("cuts")
    own = (ei // 2, ci // N, ci % N)
    core = ei % 2
    partner = ei + 1 - 2 * core
    used = [0, 0]

    def at(axis, step):
        moved = (own[axis] + step) % N
        if axis == 0:
            return (moved * 2 + core, ci)
        if axis == 1:
            return (ei, moved * N + own[2])
        return (ei, own[1] * N + moved)

    def remote(src, dst, device):
        index = used[0]
        used[0] += 1
        copy = pltpu.make_async_remote_copy(
            src_ref=src, dst_ref=dst, send_sem=send_sem.at[index], recv_sem=recv_sem.at[index],
            device_id=device, device_id_type=MESH,
        )
        copy.start()
        return copy

    def nearby(src, dst):
        index = used[1]
        used[1] += 1
        copy = pltpu.make_async_copy(src, dst, local_sem.at[index])
        copy.start()
        return copy

    def region(rest, axis, place, half, rows):
        index = [own[0], own[1], own[2]]
        index[axis] = place
        for other in rest:
            index[other] = slice(None)
        lanes = slice(None)
        if half is not None:
            if rest:
                index[min(rest)] = pl.ds(2 * half, 2)
            else:
                lanes = pl.ds(half * (FW // 2), FW // 2)
        return (*index, pl.ds(*rows), lanes)

    def gather(buf, split):
        sent = []

        def begin(colour, stage):
            axis, rest = ORDER[colour][stage], ORDER[colour][:stage]
            made = []
            for step, half in ((1, 0), (-1, 1), (1, 1), (-1, 0)):
                part = buf.at[region(rest, axis, own[axis], half, split[colour])]
                made.append(remote(part, part, at(axis, step)))
            sent.extend(made)
            return made

        going = [begin(colour, 0) for colour in range(3)]
        yield
        for stage in range(3):
            passed = []
            for colour in range(3):
                axis, rest = ORDER[colour][stage], ORDER[colour][:stage]
                going[colour][0].wait_recv()
                part = buf.at[region(rest, axis, (own[axis] - 1) % N, 0, split[colour])]
                up = remote(part, part, at(axis, 1))
                going[colour][1].wait_recv()
                part = buf.at[region(rest, axis, (own[axis] + 1) % N, 1, split[colour])]
                down = remote(part, part, at(axis, -1))
                passed.append((up, down))
                sent.extend((up, down))
            yield
            for colour in range(3):
                going[colour][2].wait_recv()
                going[colour][3].wait_recv()
                passed[colour][0].wait_recv()
                passed[colour][1].wait_recv()
                if stage < 2:
                    going[colour] = begin(colour, stage + 1)
            yield
        for copy in sent:
            copy.wait_send()
        yield

    def scatter(buf, lands, split):
        sent = []

        def land(stage, slot, half, rows):
            if stage == 0:
                return lands[0].at[slot, pl.ds(2 * half, 2), :, pl.ds(*rows), :]
            if stage == 1:
                return lands[1].at[slot, pl.ds(2 * half, 2), pl.ds(*rows), :]
            return lands[2].at[slot, pl.ds(*rows), pl.ds(half * (FW // 2), FW // 2)]

        def begin(colour, stage):
            axis, rest, rows = ORDER[colour][2 - stage], ORDER[colour][: 2 - stage], split[colour]
            made = []
            for step, far, slot, half in ((1, 2, 0, 0), (-1, 2, 0, 1), (1, 1, 1, 1), (-1, -1, 2, 0)):
                part = buf.at[region(rest, axis, (own[axis] + far) % N, half, rows)]
                made.append(remote(part, land(stage, slot, half, rows), at(axis, step)))
            sent.extend(made)
            return made

        def pieces(colour, stage, place, first, count):
            axis, rest, rows = ORDER[colour][2 - stage], ORDER[colour][: 2 - stage], split[colour]
            outer = sorted(rest)

            def one(i):
                index = [own[0], own[1], own[2]]
                index[axis] = place
                if stage == 0:
                    index[outer[0]], index[outer[1]] = i // N, i % N
                    where = (i // N, i % N)
                elif stage == 1:
                    index[outer[0]] = i
                    where = (i,)
                else:
                    where = ()
                return (*index, pl.ds(*rows)), (*where, pl.ds(*rows))

            return one

        def add_half(colour, stage, place, half):
            one = pieces(colour, stage, place, 0, 0)
            if stage == 2:
                lanes = pl.ds(half * (FW // 2), FW // 2)
                here, there = one(0)
                total = buf[(*here, lanes)].astype(F32) + lands[2][(0, *there, lanes)].astype(F32)
                buf[(*here, lanes)] = total.astype(BF)
                return
            count = 8 if stage == 0 else 2

            def body(i, carry):
                here, there = one(i + half * count)
                total = buf[(*here, slice(None))].astype(F32) + lands[stage][(0, *there, slice(None))].astype(F32)
                buf[(*here, slice(None))] = total.astype(BF)
                return carry

            lax.fori_loop(0, count, body, 0)

        def add_own(colour, stage):
            axis = ORDER[colour][2 - stage]
            one = pieces(colour, stage, own[axis], 0, 0)

            def body(i, carry):
                here, there = one(i)
                total = (
                    buf[(*here, slice(None))].astype(F32)
                    + lands[stage][(1, *there, slice(None))].astype(F32)
                    + lands[stage][(2, *there, slice(None))].astype(F32)
                )
                buf[(*here, slice(None))] = total.astype(BF)
                return carry

            if stage == 2:
                body(0, 0)
            else:
                lax.fori_loop(0, 16 if stage == 0 else 4, body, 0)

        going = [begin(colour, 0) for colour in range(3)]
        yield
        for stage in range(3):
            passed = []
            for colour in range(3):
                axis, rest, rows = ORDER[colour][2 - stage], ORDER[colour][: 2 - stage], split[colour]
                going[colour][0].wait_recv()
                place = (own[axis] + 1) % N
                add_half(colour, stage, place, 0)
                up = remote(buf.at[region(rest, axis, place, 0, rows)], land(stage, 1, 0, rows), at(axis, 1))
                going[colour][1].wait_recv()
                place = (own[axis] - 1) % N
                add_half(colour, stage, place, 1)
                down = remote(buf.at[region(rest, axis, place, 1, rows)], land(stage, 2, 1, rows), at(axis, -1))
                passed.append((up, down))
                sent.extend((up, down))
            yield
            for colour in range(3):
                going[colour][2].wait_recv()
                going[colour][3].wait_recv()
                passed[colour][0].wait_recv()
                passed[colour][1].wait_recv()
                add_own(colour, stage)
                if stage < 2:
                    going[colour] = begin(colour, stage + 1)
            yield
        for copy in sent:
            copy.wait_send()
        yield

    load_x = nearby(x_in, gx.at[own])
    load_c = nearby(c_in, gc.at[own])
    load_wg = nearby(wg_in, wg)
    load_wu = nearby(wu_in, wu)
    load_wd = nearby(wd_in, wd)
    peers = [((ei + step) % 8, ci) for step in range(1, 8)]
    peers += [at(1, step) for step in (1, 2, 3)] + [at(2, step) for step in (1, 2, 3)]
    barrier = pltpu.get_barrier_semaphore()
    for device in peers:
        pl.semaphore_signal(barrier, inc=1, device_id=device, device_id_type=MESH)
    pl.semaphore_wait(barrier, len(peers))

    load_x.wait()
    tokens = gather(gx, ROWS_X)
    next(tokens)
    load_c.wait()
    cotangents = gather(gc, ROWS_C)
    next(cotangents)

    sub = lax.broadcasted_iota(jnp.int32, (TB, TB), 0)
    lane = lax.broadcasted_iota(jnp.int32, (TB, TB), 1)
    eye = sub == lane

    def to_row(column):
        return jnp.sum(jnp.where(eye, jnp.broadcast_to(column, (TB, TB)), 0.0), axis=0, keepdims=True)

    route = route_in[...].astype(F32)
    gates = gates_in[...]
    lane_f = lane.astype(F32)
    first = (route[:, 0:1] == lane_f).astype(F32)
    second = (route[:, 1:2] == lane_f).astype(F32)
    before = dot((lane < sub).astype(BF), (first + second).astype(BF))
    goal0 = route[:, 0:1] * SLOT + jnp.sum(first * before, axis=1, keepdims=True)
    goal1 = route[:, 1:2] * SLOT + jnp.sum(second * before, axis=1, keepdims=True)
    mine[...] = jnp.zeros((8, TB), F32)
    mine[0:1, :] = to_row(goal0)
    mine[1:2, :] = to_row(goal1)
    mine[2:3, :] = to_row(gates[:, 0:1])
    mine[3:4, :] = to_row(gates[:, 1:2])
    meta[ei] = mine[...]
    told = [remote(mine, meta.at[ei], ((ei + step) % 8, ci)) for step in range(1, 8)]

    next(tokens)
    next(cotangents)
    next(tokens)
    next(cotangents)
    next(tokens)
    next(cotangents)
    next(tokens)

    for copy in told:
        copy.wait()
    slot_f = jnp.where(sub < SLOT, ei * SLOT + sub, partner * SLOT + sub - SLOT).astype(F32)
    for x in range(N):
        block = 2 * x + core
        table = meta[block]
        chosen = ((table[0:1] == slot_f) | (table[1:2] == slot_f)).astype(F32)
        pick[x] = chosen.astype(BF)
        back[x] = chosen.T.astype(BF)
    own_f = (ei * SLOT + lax.broadcasted_iota(jnp.int32, (SLOT, TB), 0)).astype(F32)
    for group in range(8):
        block = 2 * (group % N) + (core if group < N else 1 - core)
        table = meta[block]
        weight = jnp.sum(
            jnp.where(table[0:1] == own_f, table[2:3], 0.0) + jnp.where(table[1:2] == own_f, table[3:4], 0.0),
            axis=1, keepdims=True,
        )
        gslot[pl.ds(group * SLOT, SLOT), :] = jnp.broadcast_to(weight, (SLOT, TB))

    next(tokens)
    next(cotangents)
    next(tokens)
    next(tokens)

    def compact(buf, stage_buf, rows, x):
        def body(i, carry):
            y, z = i // N, i % N
            got = dot(pick[x], buf[x, y, z]).astype(BF)
            rows[y, z, pl.ds(x * SLOT, SLOT), :] = got[:SLOT]
            stage_buf[x, y, z] = got[SLOT:]
            return carry

        lax.fori_loop(0, 16, body, 0, unroll=2)
        return remote(stage_buf.at[x], rows.at[:, :, pl.ds((N + x) * SLOT, SLOT), :], (partner, ci))

    swap_x = [compact(gx, sx, xr, x) for x in range(N)]
    next(cotangents)
    load_wg.wait()
    load_wu.wait()

    def products(half):
        rows = pl.ds(half * 256, 256)

        def body(y, carry):
            up = down = None
            for z in range(N):
                block = xr[y, z, rows, :]
                feature = pl.ds(pl.multiple_of((y * N + z) * FW, FW), FW)
                g, u = dot(block, wg[feature, :]), dot(block, wu[feature, :])
                up, down = (g, u) if up is None else (up + g, down + u)
            fa[rows, :] += up
            fb[rows, :] += down
            return carry

        fa[rows, :] = jnp.zeros((256, HID), F32)
        fb[rows, :] = jnp.zeros((256, HID), F32)
        lax.fori_loop(0, N, body, 0)

    products(0)
    for copy in swap_x:
        copy.wait()
    products(1)

    def activate(i, carry):
        rows = pl.ds(pl.multiple_of(i * 32, 32), 32)
        gate, up = fa[rows, :], fb[rows, :]
        s = jax.nn.sigmoid(gate)
        act = gate * s
        value = act * up
        fh[rows, :] = value
        hid[rows, :] = (value * gslot[rows, 0:1]).astype(BF)
        fa[rows, :] = up * s * (1.0 + gate * (1.0 - s))
        fb[rows, :] = act
        return carry

    lax.fori_loop(0, 16, activate, 0)
    load_wd.wait()

    def spread(buf, stage_buf, y, value):
        def body(z, carry):
            got = value(y, z).astype(BF)
            for x in range(N):
                buf[x, y, z, 0:SLOT, :] = got[x * SLOT:(x + 1) * SLOT]
                stage_buf[x, y, z] = got[(N + x) * SLOT:(N + x + 1) * SLOT]
            return carry

        lax.fori_loop(0, N, body, 0)
        return remote(stage_buf.at[:, y], buf.at[:, y, :, pl.ds(SLOT, SLOT), :], (partner, ci))

    def forward(y, z):
        return dot(hid[...], wd[:, pl.ds(pl.multiple_of((y * N + z) * FW, FW), FW)])

    swap_m = [spread(gx, sx, y, forward) for y in range(N)]

    next(cotangents)
    next(cotangents)
    swap_c = [compact(gc, sc, dr, x) for x in range(N)]

    def expand(buf, y):
        def body(i, carry):
            x, z = i // N, i % N
            buf[x, y, z] = dot(back[x], buf[x, y, z]).astype(BF)
            return carry

        lax.fori_loop(0, 16, body, 0, unroll=2)

    for y in range(N):
        swap_m[y].wait()
        expand(gx, y)
    combine_m = scatter(gx, (lm0, lm1, lm2), ROWS_X)
    next(combine_m)

    def hidden_grad(half):
        rows = pl.ds(half * 256, 256)

        def body(y, carry):
            total = None
            for z in range(N):
                feature = pl.ds(pl.multiple_of((y * N + z) * FW, FW), FW)
                g = dot_nt(dr[y, z, rows, :], wd[:, feature])
                total = g if total is None else total + g
            fg[rows, :] += total
            return carry

        fg[rows, :] = jnp.zeros((256, HID), F32)
        lax.fori_loop(0, N, body, 0)

    hidden_grad(0)
    for copy in swap_c:
        copy.wait()
    next(combine_m)
    hidden_grad(1)

    eye_q = eye

    def inner(j, carry):
        base = pl.multiple_of(j * TB, TB)
        terms = []
        for k in range(4):
            rows = pl.ds(pl.multiple_of(base + k * 32, 32), 32)
            plain = fg[rows, :]
            terms.append(jnp.sum(fh[rows, :] * plain, axis=1, keepdims=True))
            scaled = plain * gslot[rows, 0:1]
            ggp[rows, :] = (scaled * fa[rows, :]).astype(BF)
            gup[rows, :] = (scaled * fb[rows, :]).astype(BF)
        column = jnp.concatenate(terms, axis=0)
        row = jnp.sum(jnp.where(eye_q, jnp.broadcast_to(column, (TB, TB)), 0.0), axis=0, keepdims=True)
        qy[own[1], pl.ds(j, 1), :] = row
        return carry

    qy[own[1]] = jnp.zeros((8, TB), F32)
    for j in range(4):
        inner(j, 0)
    ask_y = [remote(qy.at[own[1]], qy.at[own[1]], at(1, step)) for step in (1, 2, 3)]
    next(combine_m)

    def rows_grad(y, z):
        feature = pl.ds(pl.multiple_of((y * N + z) * FW, FW), FW)
        total = dot_nt(ggp[...], wg[feature, :]) + dot_nt(gup[...], wu[feature, :])
        return total * gslot[:, 0:1]

    swap_g = [spread(gc, sc, y, rows_grad) for y in range(2)]
    next(combine_m)
    swap_g += [spread(gc, sc, y, rows_grad) for y in range(2, N)]
    save = [nearby(src, dst) for src, dst in ((xr, xr_out), (dr, dr_out), (hid, hid_out), (ggp, ggp_out), (gup, gup_out))]
    for y in range(N):
        swap_g[y].wait()
        expand(gc, y)
    combine_g = scatter(gc, (lg0, lg1, lg2), ROWS_C)
    next(combine_g)
    for copy in ask_y:
        copy.wait()
    qz[own[2]] = qy[0] + qy[1] + qy[2] + qy[3]
    ask_z = [remote(qz.at[own[2]], qz.at[own[2]], at(2, step)) for step in (1, 2, 3)]
    next(combine_m)
    next(combine_g)
    next(combine_m)
    next(combine_m)
    mixed_out[...] = gx[own]
    for copy in ask_z:
        copy.wait()
    qe[ei] = qz[0] + qz[1] + qz[2] + qz[3]
    ask_e = [remote(qe.at[ei], qe.at[ei], ((ei + step) % 8, ci)) for step in range(1, 8)]
    next(combine_g)
    next(combine_g)
    next(combine_g)
    for copy in ask_e:
        copy.wait()
    odd = own[0] % 2
    sums = [jnp.zeros((TB, TB), F32), jnp.zeros((TB, TB), F32)]
    slot_lane = lane - SLOT * odd
    inside = (slot_lane >= 0) & (slot_lane < SLOT)
    for e in range(8):
        line = own[0] // 2 + jnp.where(core == e % 2, 0, 2)
        row = qe[e, pl.ds(line, 1), :]
        target = (slot_lane + e * SLOT).astype(F32)
        for k, goal in enumerate((goal0, goal1)):
            sums[k] += jnp.where(inside & (goal == target), row, 0.0)
    ggate_out[:, 0:1] = jnp.sum(sums[0], axis=1, keepdims=True)
    ggate_out[:, 1:2] = jnp.sum(sums[1], axis=1, keepdims=True)
    next(combine_g)
    next(combine_g)
    next(combine_m)
    next(combine_g)
    gtok_out[...] = gc[own]
    for copy in save:
        copy.wait()


def weight_kernel(xr, dr, hid, ggp, gup, gw_out, uw_out, dw_out):
    block = xr[0, 0]
    gw_out[0] = dot_tn(block, ggp[...]).astype(BF)
    uw_out[0] = dot_tn(block, gup[...]).astype(BF)
    dw_out[0] = dot_tn(hid[...], dr[0, 0]).astype(BF)


def local(tokens, routing, gates, cotangent, w_gate, w_up, w_down):
    rows = 8 * SLOT
    features = N * N * FW
    vmem, anywhere = pl.BlockSpec(memory_space=pltpu.VMEM), pl.BlockSpec(memory_space=pl.ANY)
    grid_buf = pltpu.VMEM((N, N, N, TB, FW), BF)
    row_buf = pltpu.VMEM((N, N, rows, FW), BF)
    stage_buf = pltpu.VMEM((N, N, N, SLOT, FW), BF)
    f_buf = pltpu.VMEM((rows, HID), F32)
    h_buf = pltpu.VMEM((rows, HID), BF)
    lands = [pltpu.VMEM((3, N, N, TB, FW), BF), pltpu.VMEM((3, N, TB, FW), BF), pltpu.VMEM((3, TB, FW), BF)]
    struct = jax.ShapeDtypeStruct
    mixed, grad_tokens, grad_gates, xr, dr, hid, ggp, gup = pl.pallas_call(
        layer_kernel,
        out_shape=(
            struct((TB, FW), BF), struct((TB, FW), BF), struct((TB, 2), F32),
            struct((N, N, rows, FW), BF), struct((N, N, rows, FW), BF),
            struct((rows, HID), BF), struct((rows, HID), BF), struct((rows, HID), BF),
        ),
        in_specs=[anywhere, anywhere, vmem, vmem, anywhere, anywhere, anywhere],
        out_specs=(vmem, vmem, vmem, anywhere, anywhere, anywhere, anywhere, anywhere),
        scratch_shapes=[
            grid_buf, grid_buf, row_buf, row_buf, stage_buf, stage_buf,
            pltpu.VMEM((features, HID), BF), pltpu.VMEM((features, HID), BF), pltpu.VMEM((HID, features), BF),
            f_buf, f_buf, f_buf, f_buf, h_buf, h_buf, h_buf,
            *lands, *lands,
            pltpu.VMEM((8, 8, TB), F32), pltpu.VMEM((8, TB), F32),
            pltpu.VMEM((N, TB, TB), BF), pltpu.VMEM((N, TB, TB), BF), pltpu.VMEM((rows, TB), F32),
            pltpu.VMEM((N, 8, TB), F32), pltpu.VMEM((N, 8, TB), F32), pltpu.VMEM((8, 8, TB), F32),
            pltpu.SemaphoreType.DMA((256,)), pltpu.SemaphoreType.DMA((256,)), pltpu.SemaphoreType.DMA((16,)),
        ],
        compiler_params=pltpu.CompilerParams(collective_id=0, has_side_effects=True, vmem_limit_bytes=60 * 2**20),
        name="layer",
    )(tokens, cotangent, routing, gates, w_gate[0], w_up[0], w_down[0])
    whole = lambda c: (0, 0)
    piece = pl.BlockSpec((1, 1, rows, FW), lambda c: (c // N, c % N, 0, 0))
    small = pl.BlockSpec((rows, HID), whole)
    tall = pl.BlockSpec((1, FW, HID), lambda c: (0, c, 0))
    grad_gate_w, grad_up_w, grad_down = pl.pallas_call(
        weight_kernel,
        grid=(N * N,),
        out_shape=(struct((1, features, HID), BF), struct((1, features, HID), BF), struct((1, HID, features), BF)),
        in_specs=[piece, piece, small, small, small],
        out_specs=(tall, tall, pl.BlockSpec((1, HID, FW), lambda c: (0, 0, c))),
        name="weight_grads",
    )(xr, dr, hid, ggp, gup)
    return (mixed, grad_tokens, grad_gates, grad_gate_w, grad_up_w, grad_down)


def solution(mesh):
    return jax.shard_map(
        local,
        mesh=mesh,
        in_specs=(
            P("expert", "cuts"),
            P("expert", None),
            P("expert", None),
            P("expert", "cuts"),
            P("expert", None, "cuts"),
            P("expert", None, "cuts"),
            P("expert", "cuts", None),
        ),
        out_specs=(
            P("expert", "cuts"),
            P("expert", "cuts"),
            P("expert", None),
            P("expert", None, "cuts"),
            P("expert", None, "cuts"),
            P("expert", "cuts", None),
        ),
        check_vma=False,
    )
```

```python
import functools

import jax
import jax.numpy as jnp
from jax import lax
from jax.experimental import pallas as pl
from jax.experimental.pallas import tpu as pltpu
from jax.sharding import PartitionSpec as P

MESH = pl.DeviceIdType.MESH
BF = jnp.bfloat16
F32 = jnp.float32
N = 4
SLOT = 64
TB = 128
FW = 256
HID = 512
ORDER = ((0, 1, 2), (1, 2, 0), (2, 0, 1))
ROWS_X = ((0, 48), (48, 48), (96, 32))
ROWS_C = ((0, 48), (48, 32), (80, 48))


def dot(a, b):
    return jnp.dot(a, b, preferred_element_type=F32)


def dot_nt(a, b):
    return lax.dot_general(a, b, (((1,), (1,)), ((), ())), preferred_element_type=F32)


def dot_tn(a, b):
    return lax.dot_general(a, b, (((0,), (0,)), ((), ())), preferred_element_type=F32)


def layer_kernel(
    x_in, c_in, route_in, gates_in, wg_in, wu_in, wd_in,
    mixed_out, gtok_out, ggate_out, xr_out, dr_out, hid_out, ggp_out, gup_out,
    gx, gc, xr, dr, sx, sc, wg, wu, wd, fa, fb, fh, fg, hid, ggp, gup,
    lm0, lm1, lm2, lg0, lg1, lg2, meta, mine, pick, back, gslot, qy, qz, qe,
    send_sem, recv_sem, local_sem,
):
    ei, ci = lax.axis_index("expert"), lax.axis_index("cuts")
    own = (ei // 2, ci // N, ci % N)
    core = ei % 2
    partner = ei + 1 - 2 * core
    used = [0, 0]

    def at(axis, step):
        moved = (own[axis] + step) % N
        if axis == 0:
            return (moved * 2 + core, ci)
        if axis == 1:
            return (ei, moved * N + own[2])
        return (ei, own[1] * N + moved)

    def remote(src, dst, device):
        index = used[0]
        used[0] += 1
        copy = pltpu.make_async_remote_copy(
            src_ref=src, dst_ref=dst, send_sem=send_sem.at[index], recv_sem=recv_sem.at[index],
            device_id=device, device_id_type=MESH,
        )
        copy.start()
        return copy

    def nearby(src, dst):
        index = used[1]
        used[1] += 1
        copy = pltpu.make_async_copy(src, dst, local_sem.at[index])
        copy.start()
        return copy

    def region(rest, axis, place, half, rows):
        index = [own[0], own[1], own[2]]
        index[axis] = place
        for other in rest:
            index[other] = slice(None)
        lanes = slice(None)
        if half is not None:
            if rest:
                index[min(rest)] = pl.ds(2 * half, 2)
            else:
                lanes = pl.ds(half * (FW // 2), FW // 2)
        return (*index, pl.ds(*rows), lanes)

    def gather(buf, split):
        sent = []

        def begin(colour, stage):
            axis, rest = ORDER[colour][stage], ORDER[colour][:stage]
            made = []
            for step, half in ((1, 0), (-1, 1), (1, 1), (-1, 0)):
                part = buf.at[region(rest, axis, own[axis], half, split[colour])]
                made.append(remote(part, part, at(axis, step)))
            sent.extend(made)
            return made

        going = [begin(colour, 0) for colour in range(3)]
        yield
        for stage in range(3):
            passed = []
            for colour in range(3):
                axis, rest = ORDER[colour][stage], ORDER[colour][:stage]
                going[colour][0].wait_recv()
                part = buf.at[region(rest, axis, (own[axis] - 1) % N, 0, split[colour])]
                up = remote(part, part, at(axis, 1))
                going[colour][1].wait_recv()
                part = buf.at[region(rest, axis, (own[axis] + 1) % N, 1, split[colour])]
                down = remote(part, part, at(axis, -1))
                passed.append((up, down))
                sent.extend((up, down))
            yield
            for colour in range(3):
                going[colour][2].wait_recv()
                going[colour][3].wait_recv()
                passed[colour][0].wait_recv()
                passed[colour][1].wait_recv()
                if stage < 2:
                    going[colour] = begin(colour, stage + 1)
            yield
        for copy in sent:
            copy.wait_send()
        yield

    def scatter(buf, lands, split):
        sent = []

        def land(stage, slot, half, rows):
            if stage == 0:
                return lands[0].at[slot, pl.ds(2 * half, 2), :, pl.ds(*rows), :]
            if stage == 1:
                return lands[1].at[slot, pl.ds(2 * half, 2), pl.ds(*rows), :]
            return lands[2].at[slot, pl.ds(*rows), pl.ds(half * (FW // 2), FW // 2)]

        def begin(colour, stage):
            axis, rest, rows = ORDER[colour][2 - stage], ORDER[colour][: 2 - stage], split[colour]
            made = []
            for step, far, slot, half in ((1, 2, 0, 0), (-1, 2, 0, 1), (1, 1, 1, 1), (-1, -1, 2, 0)):
                part = buf.at[region(rest, axis, (own[axis] + far) % N, half, rows)]
                made.append(remote(part, land(stage, slot, half, rows), at(axis, step)))
            sent.extend(made)
            return made

        def pieces(colour, stage, place, first, count):
            axis, rest, rows = ORDER[colour][2 - stage], ORDER[colour][: 2 - stage], split[colour]
            outer = sorted(rest)

            def one(i):
                index = [own[0], own[1], own[2]]
                index[axis] = place
                if stage == 0:
                    index[outer[0]], index[outer[1]] = i // N, i % N
                    where = (i // N, i % N)
                elif stage == 1:
                    index[outer[0]] = i
                    where = (i,)
                else:
                    where = ()
                return (*index, pl.ds(*rows)), (*where, pl.ds(*rows))

            return one

        def add_half(colour, stage, place, half):
            one = pieces(colour, stage, place, 0, 0)
            if stage == 2:
                lanes = pl.ds(half * (FW // 2), FW // 2)
                here, there = one(0)
                total = buf[(*here, lanes)].astype(F32) + lands[2][(0, *there, lanes)].astype(F32)
                buf[(*here, lanes)] = total.astype(BF)
                return
            count = 8 if stage == 0 else 2

            def body(i, carry):
                here, there = one(i + half * count)
                total = buf[(*here, slice(None))].astype(F32) + lands[stage][(0, *there, slice(None))].astype(F32)
                buf[(*here, slice(None))] = total.astype(BF)
                return carry

            lax.fori_loop(0, count, body, 0)

        def add_own(colour, stage):
            axis = ORDER[colour][2 - stage]
            one = pieces(colour, stage, own[axis], 0, 0)

            def body(i, carry):
                here, there = one(i)
                total = (
                    buf[(*here, slice(None))].astype(F32)
                    + lands[stage][(1, *there, slice(None))].astype(F32)
                    + lands[stage][(2, *there, slice(None))].astype(F32)
                )
                buf[(*here, slice(None))] = total.astype(BF)
                return carry

            if stage == 2:
                body(0, 0)
            else:
                lax.fori_loop(0, 16 if stage == 0 else 4, body, 0)

        going = [begin(colour, 0) for colour in range(3)]
        yield
        for stage in range(3):
            passed = []
            for colour in range(3):
                axis, rest, rows = ORDER[colour][2 - stage], ORDER[colour][: 2 - stage], split[colour]
                going[colour][0].wait_recv()
                place = (own[axis] + 1) % N
                add_half(colour, stage, place, 0)
                up = remote(buf.at[region(rest, axis, place, 0, rows)], land(stage, 1, 0, rows), at(axis, 1))
                going[colour][1].wait_recv()
                place = (own[axis] - 1) % N
                add_half(colour, stage, place, 1)
                down = remote(buf.at[region(rest, axis, place, 1, rows)], land(stage, 2, 1, rows), at(axis, -1))
                passed.append((up, down))
                sent.extend((up, down))
            yield
            for colour in range(3):
                going[colour][2].wait_recv()
                going[colour][3].wait_recv()
                passed[colour][0].wait_recv()
                passed[colour][1].wait_recv()
                add_own(colour, stage)
                if stage < 2:
                    going[colour] = begin(colour, stage + 1)
            yield
        for copy in sent:
            copy.wait_send()
        yield

    load_x = nearby(x_in, gx.at[own])
    load_c = nearby(c_in, gc.at[own])
    load_wg = nearby(wg_in, wg)
    load_wu = nearby(wu_in, wu)
    load_wd = nearby(wd_in, wd)
    peers = [((ei + step) % 8, ci) for step in range(1, 8)]
    peers += [at(1, step) for step in (1, 2, 3)] + [at(2, step) for step in (1, 2, 3)]
    barrier = pltpu.get_barrier_semaphore()
    for device in peers:
        pl.semaphore_signal(barrier, inc=1, device_id=device, device_id_type=MESH)
    pl.semaphore_wait(barrier, len(peers))

    load_x.wait()
    tokens = gather(gx, ROWS_X)
    next(tokens)
    load_c.wait()
    cotangents = gather(gc, ROWS_C)
    next(cotangents)

    sub = lax.broadcasted_iota(jnp.int32, (TB, TB), 0)
    lane = lax.broadcasted_iota(jnp.int32, (TB, TB), 1)
    eye = sub == lane

    def to_row(column):
        return jnp.sum(jnp.where(eye, jnp.broadcast_to(column, (TB, TB)), 0.0), axis=0, keepdims=True)

    def to_column(row):
        return jnp.sum(jnp.where(eye, jnp.broadcast_to(row, (TB, TB)), 0.0), axis=1, keepdims=True)

    route = route_in[...].astype(F32)
    gates = gates_in[...]
    number = lax.broadcasted_iota(jnp.int32, (16, TB), 0).astype(F32)
    first = (route[0:1] == number).astype(F32)
    second = (route[1:2] == number).astype(F32)
    before = dot((first + second).astype(BF), (sub < lane).astype(BF))
    goal0 = route[0:1] * SLOT + jnp.sum(first * before, axis=0, keepdims=True)
    goal1 = route[1:2] * SLOT + jnp.sum(second * before, axis=0, keepdims=True)
    mine[...] = jnp.zeros((8, TB), F32)
    mine[0:1, :] = goal0
    mine[1:2, :] = goal1
    mine[2:3, :] = gates[0:1]
    mine[3:4, :] = gates[1:2]
    meta[ei] = mine[...]
    told = [remote(mine, meta.at[ei], ((ei + step) % 8, ci)) for step in range(1, 8)]

    next(tokens)
    next(cotangents)
    next(tokens)
    next(cotangents)
    next(tokens)
    next(cotangents)
    next(tokens)

    for copy in told:
        copy.wait()
    slot_f = jnp.where(sub < SLOT, ei * SLOT + sub, partner * SLOT + sub - SLOT).astype(F32)
    for x in range(N):
        block = 2 * x + core
        table = meta[block]
        chosen = ((table[0:1] == slot_f) | (table[1:2] == slot_f)).astype(F32)
        pick[x] = chosen.astype(BF)
        back[x] = chosen.T.astype(BF)
    own_f = (ei * SLOT + lax.broadcasted_iota(jnp.int32, (SLOT, TB), 0)).astype(F32)
    for group in range(8):
        block = 2 * (group % N) + (core if group < N else 1 - core)
        table = meta[block]
        weight = jnp.sum(
            jnp.where(table[0:1] == own_f, table[2:3], 0.0) + jnp.where(table[1:2] == own_f, table[3:4], 0.0),
            axis=1, keepdims=True,
        )
        gslot[pl.ds(group * SLOT, SLOT), :] = jnp.broadcast_to(weight, (SLOT, TB))

    next(tokens)
    next(cotangents)
    next(tokens)
    next(tokens)

    def compact(buf, stage_buf, rows, x):
        def body(y, carry):
            got = [dot(pick[x], buf[x, y, z]).astype(BF) for z in range(N)]
            for z in range(N):
                rows[y, z, pl.ds(x * SLOT, SLOT), :] = got[z][:SLOT]
                stage_buf[x, y, z] = got[z][SLOT:]
            return carry

        lax.fori_loop(0, N, body, 0)
        return remote(stage_buf.at[x], rows.at[:, :, pl.ds((N + x) * SLOT, SLOT), :], (partner, ci))

    swap_x = [compact(gx, sx, xr, x) for x in range(N)]
    next(cotangents)
    load_wg.wait()
    load_wu.wait()

    for copy in swap_x:
        copy.wait()

    def products(y, carry):
        up = down = None
        for z in range(N):
            feature = pl.ds(pl.multiple_of((y * N + z) * FW, FW), FW)
            g, u = dot(xr[y, z], wg[feature, :]), dot(xr[y, z], wu[feature, :])
            up, down = (g, u) if up is None else (up + g, down + u)
        fa[...] += up
        fb[...] += down
        return carry

    fa[...] = jnp.zeros((8 * SLOT, HID), F32)
    fb[...] = jnp.zeros((8 * SLOT, HID), F32)
    lax.fori_loop(0, N, products, 0)

    def activate(i, carry):
        rows = pl.ds(pl.multiple_of(i * 32, 32), 32)
        gate, up = fa[rows, :], fb[rows, :]
        s = jax.nn.sigmoid(gate)
        act = gate * s
        value = act * up
        fh[rows, :] = value
        hid[rows, :] = (value * gslot[rows, 0:1]).astype(BF)
        fa[rows, :] = up * s * (1.0 + gate * (1.0 - s))
        fb[rows, :] = act
        return carry

    lax.fori_loop(0, 16, activate, 0)
    load_wd.wait()

    def spread(buf, stage_buf, y, value):
        def body(z, carry):
            got = value(y, z).astype(BF)
            for x in range(N):
                buf[x, y, z, 0:SLOT, :] = got[x * SLOT:(x + 1) * SLOT]
                stage_buf[x, y, z] = got[(N + x) * SLOT:(N + x + 1) * SLOT]
            return carry

        lax.fori_loop(0, N, body, 0)
        return remote(stage_buf.at[:, y], buf.at[:, y, :, pl.ds(SLOT, SLOT), :], (partner, ci))

    def forward(y, z):
        return dot(hid[...], wd[:, pl.ds(pl.multiple_of((y * N + z) * FW, FW), FW)])

    swap_m = [spread(gx, sx, y, forward) for y in range(N)]

    next(cotangents)
    next(cotangents)
    swap_c = [compact(gc, sc, dr, x) for x in range(N)]

    def expand(buf, y):
        def body(x, carry):
            got = [dot(back[x], buf[x, y, z]).astype(BF) for z in range(N)]
            for z in range(N):
                buf[x, y, z] = got[z]
            return carry

        lax.fori_loop(0, N, body, 0)

    for y in range(N):
        swap_m[y].wait()
        expand(gx, y)
    combine_m = scatter(gx, (lm0, lm1, lm2), ROWS_X)
    next(combine_m)

    def hidden_grad(y, carry):
        total = None
        for z in range(N):
            feature = pl.ds(pl.multiple_of((y * N + z) * FW, FW), FW)
            g = dot_nt(dr[y, z], wd[:, feature])
            total = g if total is None else total + g
        fg[...] += total
        return carry

    for copy in swap_c:
        copy.wait()
    fg[...] = jnp.zeros((8 * SLOT, HID), F32)
    lax.fori_loop(0, N // 2, hidden_grad, 0)
    next(combine_m)
    lax.fori_loop(N // 2, N, hidden_grad, 0)

    def inner(j, carry):
        base = pl.multiple_of(j * TB, TB)
        terms = []
        for k in range(4):
            rows = pl.ds(pl.multiple_of(base + k * 32, 32), 32)
            plain = fg[rows, :]
            terms.append(jnp.sum(fh[rows, :] * plain, axis=1, keepdims=True))
            scaled = plain * gslot[rows, 0:1]
            ggp[rows, :] = (scaled * fa[rows, :]).astype(BF)
            gup[rows, :] = (scaled * fb[rows, :]).astype(BF)
        column = jnp.concatenate(terms, axis=0)
        row = to_row(column)
        qy[own[1], pl.ds(j, 1), :] = row
        return carry

    qy[own[1]] = jnp.zeros((8, TB), F32)
    for j in range(4):
        inner(j, 0)
    ask_y = [remote(qy.at[own[1]], qy.at[own[1]], at(1, step)) for step in (1, 2, 3)]
    next(combine_m)

    def rows_grad(y, z):
        feature = pl.ds(pl.multiple_of((y * N + z) * FW, FW), FW)
        total = dot_nt(ggp[...], wg[feature, :]) + dot_nt(gup[...], wu[feature, :])
        return total * gslot[:, 0:1]

    swap_g = [spread(gc, sc, y, rows_grad) for y in range(2)]
    next(combine_m)
    swap_g += [spread(gc, sc, y, rows_grad) for y in range(2, N)]
    save = [nearby(src, dst) for src, dst in ((xr, xr_out), (dr, dr_out), (hid, hid_out), (ggp, ggp_out), (gup, gup_out))]
    for y in range(N):
        swap_g[y].wait()
        expand(gc, y)
    combine_g = scatter(gc, (lg0, lg1, lg2), ROWS_C)
    next(combine_g)
    for copy in ask_y:
        copy.wait()
    qz[own[2]] = qy[0] + qy[1] + qy[2] + qy[3]
    ask_z = [remote(qz.at[own[2]], qz.at[own[2]], at(2, step)) for step in (1, 2, 3)]
    next(combine_m)
    next(combine_g)
    next(combine_m)
    next(combine_m)
    mixed_out[...] = gx[own]
    for copy in ask_z:
        copy.wait()
    qe[ei] = qz[0] + qz[1] + qz[2] + qz[3]
    ask_e = [remote(qe.at[ei], qe.at[ei], ((ei + step) % 8, ci)) for step in range(1, 8)]
    next(combine_g)
    next(combine_g)
    next(combine_g)
    for copy in ask_e:
        copy.wait()
    odd = own[0] % 2
    goals = (to_column(goal0), to_column(goal1))
    sums = [jnp.zeros((TB, TB), F32), jnp.zeros((TB, TB), F32)]
    slot_lane = lane - SLOT * odd
    inside = (slot_lane >= 0) & (slot_lane < SLOT)
    for e in range(8):
        line = own[0] // 2 + jnp.where(core == e % 2, 0, 2)
        row = qe[e, pl.ds(line, 1), :]
        target = (slot_lane + e * SLOT).astype(F32)
        for k, goal in enumerate(goals):
            sums[k] += jnp.where(inside & (goal == target), row, 0.0)
    ggate_out[0:1] = to_row(jnp.sum(sums[0], axis=1, keepdims=True))
    ggate_out[1:2] = to_row(jnp.sum(sums[1], axis=1, keepdims=True))
    next(combine_g)
    next(combine_g)
    next(combine_m)
    next(combine_g)
    gtok_out[...] = gc[own]
    for copy in save:
        copy.wait()


def weight_kernel(
    xr, dr, hid, ggp, gup, mixed, gtok, ggate,
    gw_out, uw_out, dw_out, mixed_out, gtok_out, ggate_out,
    both, turned,
):
    @pl.when(pl.program_id(0) == 0)
    def _():
        both[:, :HID] = ggp[...]
        both[:, HID:] = gup[...]
        turned[...] = hid[...].T
        mixed_out[...] = mixed[...]
        gtok_out[...] = gtok[...]
        ggate_out[...] = ggate[...]

    grads = dot_tn(xr[0, 0], both[...])
    gw_out[0] = grads[:, :HID].astype(BF)
    uw_out[0] = grads[:, HID:].astype(BF)
    dw_out[0] = dot(turned[...], dr[0, 0]).astype(BF)


def local(tokens, routing, gates, cotangent, w_gate, w_up, w_down):
    rows = 8 * SLOT
    features = N * N * FW
    vmem, anywhere = pl.BlockSpec(memory_space=pltpu.VMEM), pl.BlockSpec(memory_space=pl.ANY)
    grid_buf = pltpu.VMEM((N, N, N, TB, FW), BF)
    row_buf = pltpu.VMEM((N, N, rows, FW), BF)
    stage_buf = pltpu.VMEM((N, N, N, SLOT, FW), BF)
    f_buf = pltpu.VMEM((rows, HID), F32)
    h_buf = pltpu.VMEM((rows, HID), BF)
    lands = [pltpu.VMEM((3, N, N, TB, FW), BF), pltpu.VMEM((3, N, TB, FW), BF), pltpu.VMEM((3, TB, FW), BF)]
    struct = jax.ShapeDtypeStruct
    mixed, grad_tokens, grad_gates, xr, dr, hid, ggp, gup = pl.pallas_call(
        layer_kernel,
        out_shape=(
            struct((TB, FW), BF), struct((TB, FW), BF), struct((2, TB), F32),
            struct((N, N, rows, FW), BF), struct((N, N, rows, FW), BF),
            struct((rows, HID), BF), struct((rows, HID), BF), struct((rows, HID), BF),
        ),
        in_specs=[anywhere, anywhere, vmem, vmem, anywhere, anywhere, anywhere],
        out_specs=(vmem, vmem, vmem, anywhere, anywhere, anywhere, anywhere, anywhere),
        scratch_shapes=[
            grid_buf, grid_buf, row_buf, row_buf, stage_buf, stage_buf,
            pltpu.VMEM((features, HID), BF), pltpu.VMEM((features, HID), BF), pltpu.VMEM((HID, features), BF),
            f_buf, f_buf, f_buf, f_buf, h_buf, h_buf, h_buf,
            *lands, *lands,
            pltpu.VMEM((8, 8, TB), F32), pltpu.VMEM((8, TB), F32),
            pltpu.VMEM((N, TB, TB), BF), pltpu.VMEM((N, TB, TB), BF), pltpu.VMEM((rows, TB), F32),
            pltpu.VMEM((N, 8, TB), F32), pltpu.VMEM((N, 8, TB), F32), pltpu.VMEM((8, 8, TB), F32),
            pltpu.SemaphoreType.DMA((256,)), pltpu.SemaphoreType.DMA((256,)), pltpu.SemaphoreType.DMA((16,)),
        ],
        compiler_params=pltpu.CompilerParams(collective_id=0, has_side_effects=True, vmem_limit_bytes=60 * 2**20),
        name="layer",
    )(tokens, cotangent, routing.T, gates.T, w_gate[0], w_up[0], w_down[0])
    whole = lambda c: (0, 0)
    piece = pl.BlockSpec((1, 1, rows, FW), lambda c: (c // N, c % N, 0, 0))
    small = pl.BlockSpec((rows, HID), whole)
    tall = pl.BlockSpec((1, FW, HID), lambda c: (0, c, 0))
    owned = pl.BlockSpec((TB, FW), whole)
    pair = pl.BlockSpec((2, TB), whole)
    grad_gate_w, grad_up_w, grad_down, mixed, grad_tokens, grad_gates = pl.pallas_call(
        weight_kernel,
        grid=(N * N,),
        out_shape=(
            struct((1, features, HID), BF), struct((1, features, HID), BF), struct((1, HID, features), BF),
            struct((TB, FW), BF), struct((TB, FW), BF), struct((2, TB), F32),
        ),
        in_specs=[piece, piece, small, small, small, owned, owned, pair],
        out_specs=(tall, tall, pl.BlockSpec((1, HID, FW), lambda c: (0, 0, c)), owned, owned, pair),
        scratch_shapes=[pltpu.VMEM((rows, 2 * HID), BF), pltpu.VMEM((HID, rows), BF)],
        name="weight_grads",
    )(xr, dr, hid, ggp, gup, mixed, grad_tokens, grad_gates)
    return (mixed, grad_tokens, grad_gates.T, grad_gate_w, grad_up_w, grad_down)


def solution(mesh):
    return jax.shard_map(
        local,
        mesh=mesh,
        in_specs=(
            P("expert", "cuts"),
            P("expert", None),
            P("expert", None),
            P("expert", "cuts"),
            P("expert", None, "cuts"),
            P("expert", None, "cuts"),
            P("expert", "cuts", None),
        ),
        out_specs=(
            P("expert", "cuts"),
            P("expert", "cuts"),
            P("expert", None),
            P("expert", None, "cuts"),
            P("expert", None, "cuts"),
            P("expert", "cuts", None),
        ),
        check_vma=False,
    )
```

```python
import functools

import jax
import jax.numpy as jnp
from jax import lax
from jax.experimental import pallas as pl
from jax.experimental.pallas import tpu as pltpu
from jax.sharding import PartitionSpec as P

MESH = pl.DeviceIdType.MESH
BF = jnp.bfloat16
F32 = jnp.float32
N = 4
SLOT = 64
TB = 128
FW = 256
HID = 512
ORDER = ((0, 1, 2), (1, 2, 0), (2, 0, 1))
ROWS_X = ((0, 48), (48, 48), (96, 32))
ROWS_C = ((0, 48), (48, 32), (80, 48))


def dot(a, b):
    return jnp.dot(a, b, preferred_element_type=F32)


def dot_nt(a, b):
    return lax.dot_general(a, b, (((1,), (1,)), ((), ())), preferred_element_type=F32)


def dot_tn(a, b):
    return lax.dot_general(a, b, (((0,), (0,)), ((), ())), preferred_element_type=F32)


def layer_kernel(
    x_in, c_in, route_in, gates_in, wg_in, wu_in, wd_in,
    mixed_out, gtok_out, ggate_out, xr_out, dr_out, hid_out, ggp_out, gup_out,
    gx, gc, xr, dr, sx, sc, wg, wu, wd, fa, fb, fh, fg, hid, ggp, gup,
    lm0, lm1, lm2, lg0, lg1, lg2, meta, mine, pick, back, gslot, qy, qz, qe,
    send_sem, recv_sem, local_sem,
):
    ei, ci = lax.axis_index("expert"), lax.axis_index("cuts")
    own = (ei // 2, ci // N, ci % N)
    core = ei % 2
    partner = ei + 1 - 2 * core
    used = [0, 0]

    def at(axis, step):
        moved = (own[axis] + step) % N
        if axis == 0:
            return (moved * 2 + core, ci)
        if axis == 1:
            return (ei, moved * N + own[2])
        return (ei, own[1] * N + moved)

    def remote(src, dst, device):
        index = used[0]
        used[0] += 1
        copy = pltpu.make_async_remote_copy(
            src_ref=src, dst_ref=dst, send_sem=send_sem.at[index], recv_sem=recv_sem.at[index],
            device_id=device, device_id_type=MESH,
        )
        copy.start()
        return copy

    def nearby(src, dst):
        index = used[1]
        used[1] += 1
        copy = pltpu.make_async_copy(src, dst, local_sem.at[index])
        copy.start()
        return copy

    def region(rest, axis, place, half, rows):
        index = [own[0], own[1], own[2]]
        index[axis] = place
        for other in rest:
            index[other] = slice(None)
        lanes = slice(None)
        if half is not None:
            if rest:
                index[min(rest)] = pl.ds(2 * half, 2)
            else:
                lanes = pl.ds(half * (FW // 2), FW // 2)
        return (*index, pl.ds(*rows), lanes)

    def gather(buf, split):
        sent = []

        def begin(colour, stage):
            axis, rest = ORDER[colour][stage], ORDER[colour][:stage]
            made = []
            for step, half in ((1, 0), (-1, 1), (1, 1), (-1, 0)):
                part = buf.at[region(rest, axis, own[axis], half, split[colour])]
                made.append(remote(part, part, at(axis, step)))
            sent.extend(made)
            return made

        going = [begin(colour, 0) for colour in range(3)]
        yield
        for stage in range(3):
            passed = []
            for colour in range(3):
                axis, rest = ORDER[colour][stage], ORDER[colour][:stage]
                going[colour][0].wait_recv()
                part = buf.at[region(rest, axis, (own[axis] - 1) % N, 0, split[colour])]
                up = remote(part, part, at(axis, 1))
                going[colour][1].wait_recv()
                part = buf.at[region(rest, axis, (own[axis] + 1) % N, 1, split[colour])]
                down = remote(part, part, at(axis, -1))
                passed.append((up, down))
                sent.extend((up, down))
            yield
            for colour in range(3):
                going[colour][2].wait_recv()
                going[colour][3].wait_recv()
                passed[colour][0].wait_recv()
                passed[colour][1].wait_recv()
                if stage < 2:
                    going[colour] = begin(colour, stage + 1)
            yield
        for copy in sent:
            copy.wait_send()
        yield

    def scatter(buf, lands, split):
        sent = []

        def land(stage, slot, half, rows):
            if stage == 0:
                return lands[0].at[slot, pl.ds(2 * half, 2), :, pl.ds(*rows), :]
            if stage == 1:
                return lands[1].at[slot, pl.ds(2 * half, 2), pl.ds(*rows), :]
            return lands[2].at[slot, pl.ds(*rows), pl.ds(half * (FW // 2), FW // 2)]

        def begin(colour, stage):
            axis, rest, rows = ORDER[colour][2 - stage], ORDER[colour][: 2 - stage], split[colour]
            made = []
            for step, far, slot, half in ((1, 2, 0, 0), (-1, 2, 0, 1), (1, 1, 1, 1), (-1, -1, 2, 0)):
                part = buf.at[region(rest, axis, (own[axis] + far) % N, half, rows)]
                made.append(remote(part, land(stage, slot, half, rows), at(axis, step)))
            sent.extend(made)
            return made

        def pieces(colour, stage, place, first, count):
            axis, rest, rows = ORDER[colour][2 - stage], ORDER[colour][: 2 - stage], split[colour]
            outer = sorted(rest)

            def one(i):
                index = [own[0], own[1], own[2]]
                index[axis] = place
                if stage == 0:
                    index[outer[0]], index[outer[1]] = i // N, i % N
                    where = (i // N, i % N)
                elif stage == 1:
                    index[outer[0]] = i
                    where = (i,)
                else:
                    where = ()
                return (*index, pl.ds(*rows)), (*where, pl.ds(*rows))

            return one

        def add_half(colour, stage, place, half):
            one = pieces(colour, stage, place, 0, 0)
            if stage == 2:
                lanes = pl.ds(half * (FW // 2), FW // 2)
                here, there = one(0)
                total = buf[(*here, lanes)].astype(F32) + lands[2][(0, *there, lanes)].astype(F32)
                buf[(*here, lanes)] = total.astype(BF)
                return
            count = 8 if stage == 0 else 2

            def body(i, carry):
                here, there = one(i + half * count)
                total = buf[(*here, slice(None))].astype(F32) + lands[stage][(0, *there, slice(None))].astype(F32)
                buf[(*here, slice(None))] = total.astype(BF)
                return carry

            lax.fori_loop(0, count, body, 0)

        def add_own(colour, stage):
            axis = ORDER[colour][2 - stage]
            one = pieces(colour, stage, own[axis], 0, 0)

            def body(i, carry):
                here, there = one(i)
                total = (
                    buf[(*here, slice(None))].astype(F32)
                    + lands[stage][(1, *there, slice(None))].astype(F32)
                    + lands[stage][(2, *there, slice(None))].astype(F32)
                )
                buf[(*here, slice(None))] = total.astype(BF)
                return carry

            if stage == 2:
                body(0, 0)
            else:
                lax.fori_loop(0, 16 if stage == 0 else 4, body, 0)

        going = [begin(colour, 0) for colour in range(3)]
        yield
        for stage in range(3):
            passed = []
            for colour in range(3):
                axis, rest, rows = ORDER[colour][2 - stage], ORDER[colour][: 2 - stage], split[colour]
                going[colour][0].wait_recv()
                place = (own[axis] + 1) % N
                add_half(colour, stage, place, 0)
                up = remote(buf.at[region(rest, axis, place, 0, rows)], land(stage, 1, 0, rows), at(axis, 1))
                going[colour][1].wait_recv()
                place = (own[axis] - 1) % N
                add_half(colour, stage, place, 1)
                down = remote(buf.at[region(rest, axis, place, 1, rows)], land(stage, 2, 1, rows), at(axis, -1))
                passed.append((up, down))
                sent.extend((up, down))
            yield
            for colour in range(3):
                going[colour][2].wait_recv()
                going[colour][3].wait_recv()
                passed[colour][0].wait_recv()
                passed[colour][1].wait_recv()
                add_own(colour, stage)
                if stage < 2:
                    going[colour] = begin(colour, stage + 1)
            yield
        for copy in sent:
            copy.wait_send()
        yield

    load_x = nearby(x_in, gx.at[own])
    load_c = nearby(c_in, gc.at[own])
    load_wg = nearby(wg_in, wg)
    load_wu = nearby(wu_in, wu)
    load_wd = nearby(wd_in, wd)
    peers = [((ei + step) % 8, ci) for step in range(1, 8)]
    peers += [at(1, step) for step in (1, 2, 3)] + [at(2, step) for step in (1, 2, 3)]
    barrier = pltpu.get_barrier_semaphore()
    for device in peers:
        pl.semaphore_signal(barrier, inc=1, device_id=device, device_id_type=MESH)
    pl.semaphore_wait(barrier, len(peers))

    load_x.wait()
    tokens = gather(gx, ROWS_X)
    next(tokens)
    load_c.wait()
    cotangents = gather(gc, ROWS_C)
    next(cotangents)

    sub = lax.broadcasted_iota(jnp.int32, (TB, TB), 0)
    lane = lax.broadcasted_iota(jnp.int32, (TB, TB), 1)
    eye = sub == lane

    def to_row(column):
        return jnp.sum(jnp.where(eye, jnp.broadcast_to(column, (TB, TB)), 0.0), axis=0, keepdims=True)

    def to_column(row):
        return jnp.sum(jnp.where(eye, jnp.broadcast_to(row, (TB, TB)), 0.0), axis=1, keepdims=True)

    route = route_in[...].astype(F32)
    gates = gates_in[...]
    number = lax.broadcasted_iota(jnp.int32, (16, TB), 0).astype(F32)
    first = (route[0:1] == number).astype(F32)
    second = (route[1:2] == number).astype(F32)
    before = dot((first + second).astype(BF), (sub < lane).astype(BF))
    goal0 = route[0:1] * SLOT + jnp.sum(first * before, axis=0, keepdims=True)
    goal1 = route[1:2] * SLOT + jnp.sum(second * before, axis=0, keepdims=True)
    mine[...] = jnp.zeros((8, TB), F32)
    mine[0:1, :] = goal0
    mine[1:2, :] = goal1
    mine[2:3, :] = gates[0:1]
    mine[3:4, :] = gates[1:2]
    meta[ei] = mine[...]
    told = [remote(mine, meta.at[ei], ((ei + step) % 8, ci)) for step in range(1, 8)]

    next(tokens)
    next(cotangents)
    next(tokens)
    next(cotangents)
    next(tokens)
    next(cotangents)
    next(tokens)

    for copy in told:
        copy.wait()
    slot_f = jnp.where(sub < SLOT, ei * SLOT + sub, partner * SLOT + sub - SLOT).astype(F32)
    for x in range(N):
        block = 2 * x + core
        table = meta[block]
        chosen = ((table[0:1] == slot_f) | (table[1:2] == slot_f)).astype(F32)
        pick[x] = chosen.astype(BF)
        back[x] = chosen.T.astype(BF)
    own_f = (ei * SLOT + lax.broadcasted_iota(jnp.int32, (SLOT, TB), 0)).astype(F32)
    for group in range(8):
        block = 2 * (group % N) + (core if group < N else 1 - core)
        table = meta[block]
        weight = jnp.sum(
            jnp.where(table[0:1] == own_f, table[2:3], 0.0) + jnp.where(table[1:2] == own_f, table[3:4], 0.0),
            axis=1, keepdims=True,
        )
        gslot[pl.ds(group * SLOT, SLOT), :] = jnp.broadcast_to(weight, (SLOT, TB))

    next(tokens)
    next(cotangents)
    next(tokens)
    next(tokens)

    def compact(buf, stage_buf, rows, x):
        chooser = pick[x]
        for y in range(N):
            for z in range(N):
                got = dot(chooser, buf[x, y, z]).astype(BF)
                rows[y, z, x * SLOT:(x + 1) * SLOT, :] = got[:SLOT]
                stage_buf[x, y, z] = got[SLOT:]
        return remote(stage_buf.at[x], rows.at[:, :, pl.ds((N + x) * SLOT, SLOT), :], (partner, ci))

    swap_x = [compact(gx, sx, xr, x) for x in range(N)]
    next(cotangents)
    load_wg.wait()
    load_wu.wait()

    for copy in swap_x:
        copy.wait()

    def products(y, carry):
        up = down = None
        for z in range(N):
            feature = pl.ds(pl.multiple_of((y * N + z) * FW, FW), FW)
            g, u = dot(xr[y, z], wg[feature, :]), dot(xr[y, z], wu[feature, :])
            up, down = (g, u) if up is None else (up + g, down + u)
        fa[...] += up
        fb[...] += down
        return carry

    fa[...] = jnp.zeros((8 * SLOT, HID), F32)
    fb[...] = jnp.zeros((8 * SLOT, HID), F32)
    lax.fori_loop(0, N, products, 0)

    def activate(i, carry):
        rows = pl.ds(pl.multiple_of(i * 32, 32), 32)
        gate, up = fa[rows, :], fb[rows, :]
        s = jax.nn.sigmoid(gate)
        act = gate * s
        value = act * up
        fh[rows, :] = value
        hid[rows, :] = (value * gslot[rows, 0:1]).astype(BF)
        fa[rows, :] = up * s * (1.0 + gate * (1.0 - s))
        fb[rows, :] = act
        return carry

    lax.fori_loop(0, 16, activate, 0)
    load_wd.wait()

    def spread(buf, stage_buf, y, value):
        def body(z, carry):
            got = value(y, z).astype(BF)
            for x in range(N):
                buf[x, y, z, 0:SLOT, :] = got[x * SLOT:(x + 1) * SLOT]
                stage_buf[x, y, z] = got[(N + x) * SLOT:(N + x + 1) * SLOT]
            return carry

        lax.fori_loop(0, N, body, 0)
        return remote(stage_buf.at[:, y], buf.at[:, y, :, pl.ds(SLOT, SLOT), :], (partner, ci))

    def forward(y, z):
        return dot(hid[...], wd[:, pl.ds(pl.multiple_of((y * N + z) * FW, FW), FW)])

    swap_m = [spread(gx, sx, y, forward) for y in range(N)]

    next(cotangents)
    next(cotangents)
    swap_c = [compact(gc, sc, dr, x) for x in range(N)]

    def expand(buf, y):
        for x in range(N):
            spreader = back[x]
            for z in range(N):
                buf[x, y, z] = dot(spreader, buf[x, y, z]).astype(BF)

    for y in range(N):
        swap_m[y].wait()
        expand(gx, y)
    combine_m = scatter(gx, (lm0, lm1, lm2), ROWS_X)
    next(combine_m)

    def hidden_grad(y, carry):
        total = None
        for z in range(N):
            feature = pl.ds(pl.multiple_of((y * N + z) * FW, FW), FW)
            g = dot_nt(dr[y, z], wd[:, feature])
            total = g if total is None else total + g
        fg[...] += total
        return carry

    for copy in swap_c:
        copy.wait()
    fg[...] = jnp.zeros((8 * SLOT, HID), F32)
    lax.fori_loop(0, N, hidden_grad, 0)

    def inner(j, carry):
        base = pl.multiple_of(j * TB, TB)
        terms = []
        for k in range(4):
            rows = pl.ds(pl.multiple_of(base + k * 32, 32), 32)
            plain = fg[rows, :]
            terms.append(jnp.sum(fh[rows, :] * plain, axis=1, keepdims=True))
            scaled = plain * gslot[rows, 0:1]
            ggp[rows, :] = (scaled * fa[rows, :]).astype(BF)
            gup[rows, :] = (scaled * fb[rows, :]).astype(BF)
        column = jnp.concatenate(terms, axis=0)
        row = to_row(column)
        qy[own[1], pl.ds(j, 1), :] = row
        return carry

    qy[own[1]] = jnp.zeros((8, TB), F32)
    for j in range(4):
        inner(j, 0)
    ask_y = [remote(qy.at[own[1]], qy.at[own[1]], at(1, step)) for step in (1, 2, 3)]
    next(combine_m)

    def rows_grad(y, z):
        feature = pl.ds(pl.multiple_of((y * N + z) * FW, FW), FW)
        total = dot_nt(ggp[...], wg[feature, :]) + dot_nt(gup[...], wu[feature, :])
        return total * gslot[:, 0:1]

    swap_g = [spread(gc, sc, y, rows_grad) for y in range(N)]
    save = [nearby(src, dst) for src, dst in ((xr, xr_out), (dr, dr_out), (hid, hid_out), (ggp, ggp_out), (gup, gup_out))]
    next(combine_m)
    for y in range(N):
        swap_g[y].wait()
        expand(gc, y)
    combine_g = scatter(gc, (lg0, lg1, lg2), ROWS_C)
    next(combine_g)
    next(combine_m)
    for copy in ask_y:
        copy.wait()
    qz[own[2]] = qy[0] + qy[1] + qy[2] + qy[3]
    ask_z = [remote(qz.at[own[2]], qz.at[own[2]], at(2, step)) for step in (1, 2, 3)]
    next(combine_m)
    next(combine_g)
    next(combine_m)
    next(combine_m)
    mixed_out[...] = gx[own]
    for copy in ask_z:
        copy.wait()
    qe[ei] = qz[0] + qz[1] + qz[2] + qz[3]
    ask_e = [remote(qe.at[ei], qe.at[ei], ((ei + step) % 8, ci)) for step in range(1, 8)]
    next(combine_g)
    next(combine_g)
    next(combine_g)
    for copy in ask_e:
        copy.wait()
    odd = own[0] % 2
    goals = (to_column(goal0), to_column(goal1))
    sums = [jnp.zeros((TB, TB), F32), jnp.zeros((TB, TB), F32)]
    slot_lane = lane - SLOT * odd
    inside = (slot_lane >= 0) & (slot_lane < SLOT)
    for e in range(8):
        line = own[0] // 2 + jnp.where(core == e % 2, 0, 2)
        row = qe[e, pl.ds(line, 1), :]
        target = (slot_lane + e * SLOT).astype(F32)
        for k, goal in enumerate(goals):
            sums[k] += jnp.where(inside & (goal == target), row, 0.0)
    ggate_out[0:1] = to_row(jnp.sum(sums[0], axis=1, keepdims=True))
    ggate_out[1:2] = to_row(jnp.sum(sums[1], axis=1, keepdims=True))
    next(combine_g)
    next(combine_g)
    next(combine_m)
    next(combine_g)
    gtok_out[...] = gc[own]
    for copy in save:
        copy.wait()


def weight_kernel(
    xr, dr, hid, ggp, gup, mixed, gtok, ggate,
    gw_out, uw_out, dw_out, mixed_out, gtok_out, ggate_out,
    both, turned,
):
    @pl.when(pl.program_id(0) == 0)
    def _():
        both[:, :HID] = ggp[...]
        both[:, HID:] = gup[...]
        turned[...] = hid[...].T
        mixed_out[...] = mixed[...]
        gtok_out[...] = gtok[...]
        ggate_out[...] = ggate[...]

    for z in range(N):
        part = slice(z * FW, (z + 1) * FW)
        grads = dot_tn(xr[0, z], both[...])
        gw_out[0, part] = grads[:, :HID].astype(BF)
        uw_out[0, part] = grads[:, HID:].astype(BF)
        dw_out[0, :, part] = dot(turned[...], dr[0, z]).astype(BF)


def local(tokens, routing, gates, cotangent, w_gate, w_up, w_down):
    rows = 8 * SLOT
    features = N * N * FW
    vmem, anywhere = pl.BlockSpec(memory_space=pltpu.VMEM), pl.BlockSpec(memory_space=pl.ANY)
    grid_buf = pltpu.VMEM((N, N, N, TB, FW), BF)
    row_buf = pltpu.VMEM((N, N, rows, FW), BF)
    stage_buf = pltpu.VMEM((N, N, N, SLOT, FW), BF)
    f_buf = pltpu.VMEM((rows, HID), F32)
    h_buf = pltpu.VMEM((rows, HID), BF)
    lands = [pltpu.VMEM((3, N, N, TB, FW), BF), pltpu.VMEM((3, N, TB, FW), BF), pltpu.VMEM((3, TB, FW), BF)]
    struct = jax.ShapeDtypeStruct
    mixed, grad_tokens, grad_gates, xr, dr, hid, ggp, gup = pl.pallas_call(
        layer_kernel,
        out_shape=(
            struct((TB, FW), BF), struct((TB, FW), BF), struct((2, TB), F32),
            struct((N, N, rows, FW), BF), struct((N, N, rows, FW), BF),
            struct((rows, HID), BF), struct((rows, HID), BF), struct((rows, HID), BF),
        ),
        in_specs=[anywhere, anywhere, vmem, vmem, anywhere, anywhere, anywhere],
        out_specs=(vmem, vmem, vmem, anywhere, anywhere, anywhere, anywhere, anywhere),
        scratch_shapes=[
            grid_buf, grid_buf, row_buf, row_buf, stage_buf, stage_buf,
            pltpu.VMEM((features, HID), BF), pltpu.VMEM((features, HID), BF), pltpu.VMEM((HID, features), BF),
            f_buf, f_buf, f_buf, f_buf, h_buf, h_buf, h_buf,
            *lands, *lands,
            pltpu.VMEM((8, 8, TB), F32), pltpu.VMEM((8, TB), F32),
            pltpu.VMEM((N, TB, TB), BF), pltpu.VMEM((N, TB, TB), BF), pltpu.VMEM((rows, TB), F32),
            pltpu.VMEM((N, 8, TB), F32), pltpu.VMEM((N, 8, TB), F32), pltpu.VMEM((8, 8, TB), F32),
            pltpu.SemaphoreType.DMA((256,)), pltpu.SemaphoreType.DMA((256,)), pltpu.SemaphoreType.DMA((16,)),
        ],
        compiler_params=pltpu.CompilerParams(collective_id=0, has_side_effects=True, vmem_limit_bytes=60 * 2**20),
        name="layer",
    )(tokens, cotangent, routing.T, gates.T, w_gate[0], w_up[0], w_down[0])
    whole = lambda c: (0, 0)
    piece = pl.BlockSpec((1, N, rows, FW), lambda c: (c, 0, 0, 0))
    small = pl.BlockSpec((rows, HID), whole)
    tall = pl.BlockSpec((1, N * FW, HID), lambda c: (0, c, 0))
    owned = pl.BlockSpec((TB, FW), whole)
    pair = pl.BlockSpec((2, TB), whole)
    grad_gate_w, grad_up_w, grad_down, mixed, grad_tokens, grad_gates = pl.pallas_call(
        weight_kernel,
        grid=(N,),
        out_shape=(
            struct((1, features, HID), BF), struct((1, features, HID), BF), struct((1, HID, features), BF),
            struct((TB, FW), BF), struct((TB, FW), BF), struct((2, TB), F32),
        ),
        in_specs=[piece, piece, small, small, small, owned, owned, pair],
        out_specs=(tall, tall, pl.BlockSpec((1, HID, N * FW), lambda c: (0, 0, c)), owned, owned, pair),
        scratch_shapes=[pltpu.VMEM((rows, 2 * HID), BF), pltpu.VMEM((HID, rows), BF)],
        name="weight_grads",
    )(xr, dr, hid, ggp, gup, mixed, grad_tokens, grad_gates)
    return (mixed, grad_tokens, grad_gates.T, grad_gate_w, grad_up_w, grad_down)


def solution(mesh):
    return jax.shard_map(
        local,
        mesh=mesh,
        in_specs=(
            P("expert", "cuts"),
            P("expert", None),
            P("expert", None),
            P("expert", "cuts"),
            P("expert", None, "cuts"),
            P("expert", None, "cuts"),
            P("expert", "cuts", None),
        ),
        out_specs=(
            P("expert", "cuts"),
            P("expert", "cuts"),
            P("expert", None),
            P("expert", None, "cuts"),
            P("expert", None, "cuts"),
            P("expert", "cuts", None),
        ),
        check_vma=False,
    )
```
